32 devices in a mesh: lat: 4 (over y, core), lon: 8 (over z, x).
Axes of the slice: x: 2, y: 2, z: 4, core: 2. Of those that a mesh axis runs over, the one named last changes fastest.
Arguments:
- queries: bfloat16 [12, 360, 1024], P('lat', 'lon'), may hold values from -68 to 68
- keys: bfloat16 [12, 360, 1024], P('lat', 'lon'), may hold values from -6 to 6
- values: bfloat16 [12, 360, 1024], P('lat', 'lon'), may hold values from -6 to 6
- cotangent: bfloat16 [12, 360, 1024], P('lat', 'lon'), may hold values from -6 to 6
- pair_list: int32 [12, 9], replicated, may hold values from -1 to 8, as said below
- quad_index: int32 [12], replicated, may hold values from 0 to 31
- quad_table: float32 [32], replicated, may hold values from 0.1 to 1
Outputs:
- attended: bfloat16 [12, 360, 1024], P('lat', 'lon')
- grad_queries: bfloat16 [12, 360, 1024], P('lat', 'lon')
- grad_keys: bfloat16 [12, 360, 1024], P('lat', 'lon')
- grad_values: bfloat16 [12, 360, 1024], P('lat', 'lon')
The draws below stay inside these ranges and needn't reach their ends.
Inputs may be any that keep to these rules, and one draw needn't show every extreme that they name: `pair_list`: row r lists distinct codes in increasing order, then -1 in the remaining slots; code 4 (the query tile itself) is always listed, codes 1 and 7 are listed wherever the row they name lies inside 0 to 11, and no listed code names a row outside 0 to 11.
All inputs are finite; a program needn't handle non-finite values.
Results may differ from the reference program's by a relative error of at most 0.012.
The reference program's roundings to bfloat16 on the way count: a program that leaves them out, or rounds other values in their place, can miss the bound.
Values may be sent and summed in bfloat16 or wider, within the bound.
No kernel may reach another device: no remote copies, remote signals or barrier semaphores. Data moves between devices by JAX's collectives and lax.ppermute only.
A program may use at most 64 MiB of HBM per device.

```python
import math
import jax
import jax.numpy as jnp
from jax import lax

HEADS = 16
HEAD = 64
D = 1024
TILE = 45
NPAIR = 9
QTAB = 32
NLAT = 12
NLON = 360


def query_key_pair(key):
    shape_full = (NLAT, NLON, D)
    base_queries = jnp.clip(jax.random.normal(jax.random.fold_in(key, 11), shape_full, jnp.float32), -6.0, 6.0)
    base_keys = jnp.clip(jax.random.normal(jax.random.fold_in(key, 12), shape_full, jnp.float32), -6.0, 6.0)
    return (base_queries, base_keys)


def draw_queries(key, part):
    return query_key_pair(key)[0].astype(jnp.bfloat16)


def draw_keys(key, part):
    return query_key_pair(key)[1].astype(jnp.bfloat16)


def draw_pair_list(key, part):
    row_ids = jnp.arange(NLAT, dtype=jnp.int32)[:, None]
    code_ids = jnp.arange(NPAIR, dtype=jnp.int32)[None, :]
    chance = jax.random.randint(jax.random.fold_in(key, 21), (NLAT, NPAIR), 0, NLAT)
    chosen = (chance <= row_ids) | (code_ids == 4) | (code_ids == 1) | (code_ids == 7) | (row_ids == NLAT - 2)
    source = row_ids + code_ids // 3 - 1
    chosen = chosen & (source >= 0) & (source < NLAT)
    ordered = jnp.sort(jnp.where(chosen, code_ids, code_ids + 100), axis=1)
    return jnp.where(ordered < 100, ordered, -1).astype(jnp.int32)


def set_ends(values, rng, least, top_value):
    shape = values.shape
    place = [jax.random.randint(jax.random.fold_in(rng, axis), (), 0, shape[axis]) for axis in range(len(shape))]
    values = values.at[tuple(place)].set(least)
    longest = shape.index(max(shape))
    place[longest] = (place[longest] + 1) % shape[longest]
    return values.at[tuple(place)].set(top_value)


def steps_of(key, shape, shards, least, top_value):
    level, own = 1.0, jax.random.fold_in(key, 6)
    for axis_at, parts in shards:
        steps = jnp.exp(jax.random.uniform(jax.random.fold_in(own, axis_at), (parts,), jnp.float32, least / len(shards), top_value / len(shards)))
        level = level * jnp.repeat(steps, shape[axis_at] // parts).reshape([-1 if axis == axis_at else 1 for axis in range(len(shape))])
    return level


def centred(own_key, extent, width, most, split=(), held_as=jnp.bfloat16):
    level = steps_of(own_key, extent, split, -0.22, 0.18) if split else 1.0
    array = jax.random.normal(own_key, extent, jnp.float32) * width * level
    return jnp.minimum(jnp.maximum(array, -most), most).astype(held_as)


def setup_inputs(seed: int = 0) -> dict:
    key_list = jax.random.split(jax.random.key(seed), 8)
    return {
        "queries": draw_queries(jax.random.fold_in(key_list[7], 71), 0),
        "keys": draw_keys(jax.random.fold_in(key_list[7], 71), 0),
        "values": centred(key_list[2], (NLAT, NLON, D), 1.0, 6.0, ((0, 4), (1, 8))),
        "cotangent": centred(key_list[3], (NLAT, NLON, D), 1.0, 6.0, ((0, 4), (1, 8))),
        "pair_list": draw_pair_list(jax.random.fold_in(key_list[7], 71), 0),
        "quad_index": set_ends(jax.random.randint(key_list[5], (NLAT,), 0, QTAB), jax.random.fold_in(key_list[5], 1), 0, QTAB - 1).astype(jnp.int32),
        "quad_table": jnp.clip(jnp.exp(jax.random.uniform(key_list[6], (QTAB,), jnp.float32, math.log(0.1), math.log(1.0))), 0.1, 1.0),
    }


def rounded(float_values):
    return lax.optimization_barrier(float_values.astype(jnp.bfloat16)).astype(jnp.float32)

def reference(queries, keys, values, cotangent, pair_list, quad_index, quad_table):
    lat_count, lon_count, model_width = queries.shape
    tile_count = lon_count // TILE
    head_scale = HEAD ** (-0.5)
    shape_tiles = (lat_count, tile_count, TILE, HEADS, HEAD)
    q_tiles = queries.reshape(shape_tiles)
    k_tiles = keys.reshape(shape_tiles)
    v_tiles = values.reshape(shape_tiles)
    g_tiles = cotangent.reshape(shape_tiles)
    codes_all = jnp.arange(NPAIR, dtype=jnp.int32)
    lat_step = codes_all // 3 - 1
    lon_step = codes_all % 3 - 1
    member = jnp.any(pair_list[:, :, None] == codes_all[None, None, :], axis=1)
    row_weight = quad_table[quad_index]

    def gather_keys(tile_id):
        row_index = tile_id // tile_count
        col_index = tile_id % tile_count
        key_rows = jnp.clip(row_index + lat_step, 0, lat_count - 1).astype(jnp.int32)
        key_cols = ((col_index + lon_step) % tile_count).astype(jnp.int32)
        listed = member[row_index]
        weight = row_weight[key_rows]
        key_tile = k_tiles[key_rows, key_cols].astype(jnp.float32)
        value_tile = v_tiles[key_rows, key_cols].astype(jnp.float32)
        query_tile = q_tiles[row_index, col_index].astype(jnp.float32)
        grad_tile = g_tiles[row_index, col_index].astype(jnp.float32)
        return (listed, weight, key_tile, value_tile, query_tile, grad_tile)

    def forward_tile(tile_id):
        listed, weight, key_tile, value_tile, query_tile, grad_tile = gather_keys(tile_id)
        scores = jnp.einsum('qhd,ckhd->hqck', query_tile, key_tile) * head_scale
        pair_mask = listed[None, None, :, None]
        row_max = lax.optimization_barrier(jnp.max(jnp.where(pair_mask, scores, -1e+30), axis=(2, 3)))
        shares = jnp.where(pair_mask, weight[None, None, :, None] * jnp.exp(scores - row_max[:, :, None, None]), 0.0)
        row_total = lax.optimization_barrier(jnp.sum(shares, axis=(2, 3)))
        mixed_heads = jnp.einsum('hqck,ckhd->qhd', rounded(shares), value_tile) / row_total.T[:, :, None]
        attended_tile = mixed_heads.reshape(TILE, model_width).astype(jnp.bfloat16)
        attended_heads = attended_tile.astype(jnp.float32).reshape(TILE, HEADS, HEAD)
        row_delta = lax.optimization_barrier(jnp.sum(grad_tile * attended_heads, axis=-1)).T
        return (attended_tile, row_max + jnp.log(row_total), row_delta)
    tile_ids = jnp.arange(lat_count * tile_count, dtype=jnp.int32)
    attended, lse_all, delta_all = lax.map(forward_tile, tile_ids)

    def query_grad(tile_id):
        listed, weight, key_tile, value_tile, query_tile, grad_tile = gather_keys(tile_id)
        scores = jnp.einsum('qhd,ckhd->hqck', query_tile, key_tile) * head_scale
        pair_mask = listed[None, None, :, None]
        probs = jnp.where(pair_mask, weight[None, None, :, None] * jnp.exp(scores - lse_all[tile_id][:, :, None, None]), 0.0)
        grad_probs = jnp.einsum('qhd,ckhd->hqck', grad_tile, value_tile)
        slopes = rounded(probs * (grad_probs - delta_all[tile_id][:, :, None, None]))
        result = jnp.einsum('hqck,ckhd->qhd', slopes, key_tile) * head_scale
        return result.reshape(TILE, model_width).astype(jnp.bfloat16)
    grad_queries = lax.map(query_grad, tile_ids)

    def key_grad(tile_id):
        row_index = tile_id // tile_count
        col_index = tile_id % tile_count
        source_rows = row_index - lat_step
        inside = (source_rows >= 0) & (source_rows < lat_count)
        clipped = jnp.clip(source_rows, 0, lat_count - 1).astype(jnp.int32)
        source_cols = ((col_index - lon_step) % tile_count).astype(jnp.int32)
        listed = inside & member[clipped, codes_all]
        source_ids = (clipped * tile_count + source_cols).astype(jnp.int32)
        query_tile = q_tiles[clipped, source_cols].astype(jnp.float32)
        grad_tile = g_tiles[clipped, source_cols].astype(jnp.float32)
        lse_source = jnp.transpose(lse_all[source_ids], (1, 0, 2))
        delta_source = jnp.transpose(delta_all[source_ids], (1, 0, 2))
        key_tile = k_tiles[row_index, col_index].astype(jnp.float32)
        value_tile = v_tiles[row_index, col_index].astype(jnp.float32)
        weight = row_weight[row_index]
        scores = jnp.einsum('cqhd,khd->hcqk', query_tile, key_tile) * head_scale
        pair_mask = listed[None, :, None, None]
        probs = jnp.where(pair_mask, weight * jnp.exp(scores - lse_source[..., None]), 0.0)
        grad_probs = jnp.einsum('cqhd,khd->hcqk', grad_tile, value_tile)
        slopes = rounded(probs * (grad_probs - delta_source[..., None]))
        key_out = jnp.einsum('hcqk,cqhd->khd', slopes, query_tile) * head_scale
        value_out = jnp.einsum('hcqk,cqhd->khd', rounded(probs), grad_tile)
        return (key_out.reshape(TILE, model_width).astype(jnp.bfloat16), value_out.reshape(TILE, model_width).astype(jnp.bfloat16))
    grad_keys, grad_values = lax.map(key_grad, tile_ids)
    full_shape = (lat_count, lon_count, model_width)
    return (attended.reshape(full_shape), grad_queries.reshape(full_shape), grad_keys.reshape(full_shape), grad_values.reshape(full_shape))
```

```python
import functools
import jax
import jax.numpy as jnp
from jax import lax
from jax.experimental import pallas as pl
from jax.experimental.pallas import tpu as pltpu
from jax.sharding import Mesh, PartitionSpec as P

HEADS = 16
HEAD = 64
TILE = 45
NPAIR = 9
LANES = 128
SLOT = 48
LON_GROUP = 2
FAR = -1e30


def dot(a, b, da, db):
    return lax.dot_general(
        a, b, (((da,), (db,)), ((), ())), preferred_element_type=jnp.float32
    )


def attention_kernel(rows, band_rows, first_row_ref, pair_ref, quad_ref, table_ref,
                     qg_ref, kv_ref, west_ref, east_ref, cap_ref,
                     out_ref, own_ref, rim_ref, lat_ref,
                     ext, acc, weights):
    f32, bf16 = jnp.float32, jnp.bfloat16
    first_row = first_row_ref[0]
    lat_count = quad_ref.shape[0]

    def fill(r, carry):
        band, inner = r // band_rows, r % band_rows
        for kv in range(2):
            ext[kv, r + 1, 0] = west_ref[band, kv, inner]
            ext[kv, r + 1, 1] = kv_ref[band * 2, kv, inner]
            ext[kv, r + 1, 2] = kv_ref[band * 2 + 1, kv, inner]
            ext[kv, r + 1, 3] = east_ref[band, kv, inner]

        def clear(c, carry):
            weights[r * NPAIR + c] = 0.0
            return carry

        lax.fori_loop(0, NPAIR, clear, 0)

        def mark(s, carry):
            code = pair_ref[first_row + r, s]

            @pl.when(code >= 0)
            def _():
                source = jnp.clip(first_row + r + code // 3 - 1, 0, lat_count - 1)
                weights[r * NPAIR + code] = table_ref[quad_ref[source]]

            return carry

        return lax.fori_loop(0, NPAIR, mark, carry)

    lax.fori_loop(0, rows, fill, 0)
    for kv in range(2):
        for end in range(2):
            ext[kv, end * (rows + 1)] = cap_ref[end, kv]
    acc[...] = jnp.zeros_like(acc)

    half = 2 * SLOT
    width = 2 * half
    first_half = lax.broadcasted_iota(jnp.int32, (1, width), 1) < half
    low_lanes = lax.broadcasted_iota(jnp.int32, (SLOT, LANES), 1) < HEAD
    low_mask = low_lanes.astype(bf16)
    high_mask = jnp.logical_not(low_lanes).astype(bf16)
    pad_rows = jnp.where(
        lax.broadcasted_iota(jnp.int32, (8, width), 0) < TILE - (SLOT - 8), 0.0, FAR
    )
    blank = jnp.zeros((half, LANES), bf16)

    def by_head(tile):
        return jnp.concatenate([tile * low_mask, tile * high_mask], 0)

    def both(pair):
        stacked = jnp.concatenate(pair, 0)
        split = jnp.concatenate(
            [jnp.concatenate([pair[0], blank], 1), jnp.concatenate([blank, pair[1]], 1)], 0
        )
        return stacked, split

    def merge(full):
        tiles = []
        for x in range(2):
            part = full[x * half : (x + 1) * half, x * LANES : (x + 1) * LANES]
            tiles.append(jnp.where(low_lanes, part[:SLOT], part[SLOT:]))
        return tiles

    def as_column(row):
        return jnp.transpose(jnp.broadcast_to(row, (8, width)))[:, :1]

    def step(r, carry):
        band, inner = r // band_rows, r % band_rows
        q_raw = [qg_ref[band * 2 + x, 0, inner] for x in range(2)]
        g_raw = [qg_ref[band * 2 + x, 1, inner] for x in range(2)]
        q_two, q_split = both([by_head(t * jnp.asarray(HEAD**-0.5, bf16)) for t in q_raw])
        g_two, g_split = both([by_head(t) for t in g_raw])

        def gathered(kv):
            inside = [ext[kv, r + a, x] for a in range(3) for x in (1, 2)]
            inside = jnp.concatenate(inside, 0)
            rim = [
                jnp.concatenate([ext[kv, r + a, 0], ext[kv, r + a, 3]], 1) for a in range(3)
            ]
            rim = jnp.concatenate(rim, 0)
            return inside, rim, jnp.concatenate(
                [jnp.concatenate([inside, inside], 1), rim], 0
            )

        k_in, k_rim, k_all = gathered(0)
        v_in, v_rim, v_all = gathered(1)
        scores = jnp.concatenate([dot(k_in, q_two, 1, 1), dot(k_rim, q_split, 1, 1)], 0)
        grad_probs = jnp.concatenate([dot(v_in, g_two, 1, 1), dot(v_rim, g_split, 1, 1)], 0)

        def bias(a, b_first, b_second):
            w = jnp.where(
                first_half,
                weights[r * NPAIR + 3 * a + b_first + 1],
                weights[r * NPAIR + 3 * a + b_second + 1],
            )
            return jnp.where(w > 0, jnp.log(jnp.where(w > 0, w, 1.0)), FAR)

        biases = []
        for a in range(3):
            biases += [bias(a, 0, -1), bias(a, 1, 0)]
        for a in range(3):
            biases += [bias(a, -1, 1)]
        shifted = []
        for j, row in enumerate(biases):
            block = scores[j * SLOT : (j + 1) * SLOT]
            shifted += [block[: SLOT - 8] + row, block[SLOT - 8 :] + (row + pad_rows)]
        shifted = jnp.concatenate(shifted, 0)
        top = jnp.max(shifted, axis=0, keepdims=True)
        shares = jnp.exp(shifted - top)
        total = jnp.sum(shares, axis=0, keepdims=True)
        inverse = 1.0 / total
        mixed = dot(shares.astype(bf16), v_all, 0, 0)
        mixed = mixed / as_column(total)
        attended = [t.astype(bf16) for t in merge(mixed)]
        for x in range(2):
            out_ref[band * 2 + x, 0, inner] = attended[x]
        att_f = [t.astype(f32) for t in attended]
        products = jnp.concatenate(
            [g_two[: half].astype(f32) * jnp.concatenate([att_f[0]] * 2, 0),
             g_two[half:].astype(f32) * jnp.concatenate([att_f[1]] * 2, 0)], 0
        )
        delta = jnp.sum(jnp.transpose(products), axis=0, keepdims=True)
        probs = shares * inverse
        slopes = (probs * (grad_probs - delta)).astype(bf16)
        probs = probs.astype(bf16)
        dq = merge(dot(slopes, k_all, 0, 0) * HEAD**-0.5)
        for x in range(2):
            out_ref[band * 2 + x, 1, inner] = dq[x].astype(bf16)
        inside_rows = 6 * SLOT
        for kv, left, two, split in ((0, slopes, q_two, q_split), (1, probs, g_two, g_split)):
            inside = dot(left[:inside_rows], two, 1, 0)
            rim = dot(left[inside_rows:], split, 1, 0)
            for a in range(3):
                for x in range(2):
                    at = (2 * a + x) * SLOT
                    acc[kv, r + a, 1 + x] += inside[at : at + SLOT]
                at = a * SLOT
                acc[kv, r + a, 0] += rim[at : at + SLOT, :LANES]
                acc[kv, r + a, 3] += rim[at : at + SLOT, LANES:]
        return carry

    lax.fori_loop(0, rows, step, 0)

    def flush(r, carry):
        band, inner = r // band_rows, r % band_rows
        for kv in range(2):
            for x in range(2):
                own_ref[band * 2 + x, kv, inner] = acc[kv, r + 1, 1 + x]
                rim_ref[x, band, kv, inner] = acc[kv, r + 1, 3 * x].astype(bf16)
        return carry

    lax.fori_loop(0, rows, flush, 0)
    for kv in range(2):
        for end in range(2):
            lat_ref[end, kv] = acc[kv, end * (rows + 1)]


def shift(value, axis, by, wrap):
    size = lax.axis_size(axis)
    pairs = [(i, (i + by) % size) for i in range(size) if wrap or 0 <= i + by < size]
    return lax.ppermute(value, axis, pairs)


def packed(first, second):
    both = jnp.stack([first, second])
    both = jnp.pad(both, ((0, 0), (0, 0), (0, SLOT - TILE), (0, 0)))
    split = both.reshape(both.shape[:3] + (both.shape[3] // LANES, LANES))
    return split.transpose(3, 0, 1, 2, 4)


def unpacked(block):
    moved = block.transpose(1, 2, 3, 0, 4)
    joined = moved.reshape(moved.shape[:3] + (moved.shape[3] * LANES,))
    return joined[:, :, :TILE]


def on_device(queries, keys, values, cotangent, pair_list, quad_index, quad_table):
    band_rows = queries.shape[0]
    bands = lax.axis_size("lat_in")
    rows = band_rows * bands
    group = ("lat_in", "lon_in")
    lat_groups = lax.axis_size("lat_out")
    exchange = functools.partial(
        lax.all_to_all, axis_name=group, split_axis=0, concat_axis=0, tiled=True
    )
    kv = exchange(packed(keys, values))
    by_tile = kv.reshape((bands, 2) + kv.shape[1:])
    west = shift(by_tile[:, 1], "lon_out", 1, True)
    east = shift(by_tile[:, 0], "lon_out", -1, True)
    qg = exchange(packed(queries, cotangent))
    if lat_groups > 1:
        def edge(band, inner):
            tiles = [west[band, :, inner], by_tile[band, 0, :, inner],
                     by_tile[band, 1, :, inner], east[band, :, inner]]
            return jnp.stack(tiles, 1)

        north = shift(edge(bands - 1, band_rows - 1), "lat_out", 1, False)
        south = shift(edge(0, 0), "lat_out", -1, False)
        caps = jnp.stack([north, south])
        first_row = (lax.axis_index("lat_out") * rows).astype(jnp.int32).reshape(1)
    else:
        caps = jnp.zeros((2, 2, 4, SLOT, LANES), jnp.bfloat16)
        first_row = jnp.zeros((1,), jnp.int32)
    smem = pl.BlockSpec(memory_space=pltpu.SMEM)
    vmem = pl.BlockSpec(memory_space=pltpu.VMEM)
    out, own, rim, lat_rim = pl.pallas_call(
        functools.partial(attention_kernel, rows, band_rows),
        out_shape=(
            jax.ShapeDtypeStruct(qg.shape, jnp.bfloat16),
            jax.ShapeDtypeStruct(qg.shape, jnp.float32),
            jax.ShapeDtypeStruct((2,) + west.shape, jnp.bfloat16),
            jax.ShapeDtypeStruct(caps.shape, jnp.float32),
        ),
        in_specs=[smem] * 4 + [vmem] * 5,
        out_specs=(vmem,) * 4,
        scratch_shapes=[
            pltpu.VMEM((2, rows + 2, 4, SLOT, LANES), jnp.bfloat16),
            pltpu.VMEM((2, rows + 2, 4, SLOT, LANES), jnp.float32),
            pltpu.SMEM((rows * NPAIR,), jnp.float32),
        ],
        compiler_params=pltpu.CompilerParams(vmem_limit_bytes=32 * 2**20),
        name="row_attention",
    )(first_row, pair_list, quad_index, quad_table, qg, kv, west, east, caps)
    own = own.reshape((bands, 2) + own.shape[1:])
    if lat_groups > 1:
        lat_rim = lat_rim.astype(jnp.bfloat16)
        north = shift(lat_rim[1], "lat_out", 1, False).astype(jnp.float32)
        south = shift(lat_rim[0], "lat_out", -1, False).astype(jnp.float32)
        rim = rim.astype(jnp.float32)
        for band, inner, add in ((0, 0, north), (bands - 1, band_rows - 1, south)):
            own = own.at[band, :, :, inner].add(add[:, 1:3].swapaxes(0, 1))
            rim = rim.at[:, band, :, inner].add(add[:, 0::3].swapaxes(0, 1))
        rim = rim.astype(jnp.bfloat16)
    from_east = shift(rim[0], "lon_out", -1, True)
    from_west = shift(rim[1], "lon_out", 1, True)
    out = unpacked(exchange(out))
    own = own + jnp.stack([from_west, from_east], 1).astype(jnp.float32)
    grads = unpacked(exchange(own.astype(jnp.bfloat16).reshape(qg.shape)))
    return out[0], out[1], grads[0], grads[1]


def solution(mesh):
    lat, lon = mesh.shape["lat"], mesh.shape["lon"]
    lon_in = LON_GROUP
    lat_in = HEADS * HEAD // LANES // lon_in
    finer = Mesh(
        mesh.devices.reshape(lat // lat_in, lat_in, lon // lon_in, lon_in),
        ("lat_out", "lat_in", "lon_out", "lon_in"),
    )
    block = P(("lat_out", "lat_in"), ("lon_out", "lon_in"), None)
    return jax.shard_map(
        on_device,
        mesh=finer,
        in_specs=(block,) * 4 + (P(),) * 3,
        out_specs=(block,) * 4,
        check_vma=False,
    )
```

```python
import functools
import jax
import jax.numpy as jnp
from jax import lax
from jax.experimental import pallas as pl
from jax.experimental.pallas import tpu as pltpu
from jax.sharding import Mesh, PartitionSpec as P

HEADS = 16
HEAD = 64
TILE = 45
NPAIR = 9
LANES = 128
SLOT = 48
HALF = 2 * SLOT
WIDTH = 2 * HALF
LON_GROUP = 2
CHUNKS = HEADS * HEAD // LANES
ROUTES = (5, 7, 4, 6, 1, 3, 2)
FAR = -1e30
FLIGHT = 3
GROUP = ("lat_in", "lon_in")


f32, bf16 = jnp.float32, jnp.bfloat16


def dot(a, b, da, db):
    return lax.dot_general(a, b, (((da,), (db,)), ((), ())), preferred_element_type=f32)


def pack_kernel(me_ref, first_ref, second_ref, *out_refs):
    me = me_ref[0]
    for o, out_ref in enumerate(out_refs):
        lanes = pl.ds(pl.multiple_of((me ^ o) * LANES, LANES), LANES)
        for kv, ref in enumerate((first_ref, second_ref)):
            for i in range(ref.shape[0]):
                out_ref[kv, i, 32:] = jnp.zeros((SLOT - 32, LANES), bf16)
                out_ref[kv, i, :TILE] = ref[i, :, lanes]


def unpack_kernel(me_ref, *refs):
    me = me_ref[0]
    outs = refs[CHUNKS:]
    for o, block_ref in enumerate(refs[:CHUNKS]):
        lanes = pl.ds(pl.multiple_of((me ^ o) * LANES, LANES), LANES)
        for kv, ref in enumerate(outs):
            for i in range(ref.shape[0]):
                ref[i, :, lanes] = block_ref[kv, i, :TILE]


def head_masks():
    low = lax.broadcasted_iota(jnp.int32, (SLOT, LANES), 1) < HEAD
    return low, low.astype(bf16), jnp.logical_not(low).astype(bf16)


def pad_rows():
    row = lax.broadcasted_iota(jnp.int32, (8, WIDTH), 0)
    return jnp.where(row < TILE - (SLOT - 8), 0.0, FAR)


def stacked(pair, masks):
    tall = [jnp.concatenate([t * masks[1], t * masks[2]], 0) for t in pair]
    blank = jnp.zeros((HALF, LANES), bf16)
    split = [
        jnp.concatenate([tall[0], blank], 1),
        jnp.concatenate([blank, tall[1]], 1),
    ]
    return jnp.concatenate(tall, 0), jnp.concatenate(split, 0)


def biased(scores, rows, pad):
    parts = []
    for j, row in enumerate(rows):
        block = scores[j * SLOT : (j + 1) * SLOT]
        parts += [block[: SLOT - 8] + row, block[SLOT - 8 :] + (row + pad)]
    return jnp.concatenate(parts, 0)


def interleaved(line, rows):
    flight = FLIGHT if rows % FLIGHT == 0 else 1

    def step(i, carry):
        waiting = [line(i * flight + k) for k in range(flight)]
        live = []
        while waiting or live:
            if waiting:
                live.append(waiting.pop(0))
            live = [one for one in live if next(one, FAR) != FAR]
        return carry

    lax.fori_loop(0, rows // flight, step, 0)


def main_kernel(rows, band_rows, me_ref, bias_ref, qg_ref, odd_ref, even_ref, cap_ref, *refs):
    block_refs = refs[:CHUNKS]
    out_ref, acc, ext, stat_ref = refs[CHUNKS:]
    me = me_ref[0]
    side = me & 1

    def place(tile_row, tile, value):
        for kv in range(2):
            ext[kv, tile_row + 1, tile] = value[kv]

    for o, ref in enumerate(block_refs):
        source = me ^ o
        for i in range(band_rows):
            place((source >> 1) * band_rows + i, 1 + (source & 1), ref[:, i])
    for j in range(CHUNKS // 2):
        for ref, o, tile in ((odd_ref, 2 * j + 1, 3 * side), (even_ref, 2 * j, 3 - 3 * side)):
            for i in range(band_rows):
                place(((me ^ o) >> 1) * band_rows + i, tile, ref[j, :, i])
    for end in range(2):
        for kv in range(2):
            ext[kv, end * (rows + 1)] = cap_ref[end, kv]
    acc[...] = jnp.zeros_like(acc)
    masks = head_masks()
    pad = pad_rows()

    def merge(full):
        tiles = []
        for x in range(2):
            part = full[x * HALF : (x + 1) * HALF, x * LANES : (x + 1) * LANES]
            tiles.append(jnp.where(masks[0], part[:SLOT], part[SLOT:]))
        return tiles

    def as_column(row):
        return jnp.transpose(jnp.broadcast_to(row, (8, WIDTH)))[:, :1]

    def gathered(kv, r):
        inside = jnp.concatenate([ext[kv, r + a, x] for a in range(3) for x in (1, 2)], 0)
        rim = jnp.concatenate(
            [jnp.concatenate([ext[kv, r + a, 0], ext[kv, r + a, 3]], 1) for a in range(3)], 0
        )
        return inside, rim, jnp.concatenate([jnp.concatenate([inside, inside], 1), rim], 0)

    def line(r):
        band, inner = r // band_rows, r % band_rows
        scale = jnp.asarray(HEAD**-0.5, bf16)
        q_two, q_split = stacked([qg_ref[band * 2 + x, 0, inner] * scale for x in range(2)], masks)
        g_two, g_split = stacked([qg_ref[band * 2 + x, 1, inner] for x in range(2)], masks)
        k_in, k_rim, k_all = gathered(0, r)
        v_in, v_rim, v_all = gathered(1, r)
        yield
        scores = jnp.concatenate([dot(k_in, q_two, 1, 1), dot(k_rim, q_split, 1, 1)], 0)
        grad_probs = jnp.concatenate([dot(v_in, g_two, 1, 1), dot(v_rim, g_split, 1, 1)], 0)
        yield
        shifted = biased(scores, [bias_ref[r, j : j + 1] for j in range(NPAIR)], pad)
        top = jnp.max(shifted, axis=0, keepdims=True)
        yield
        shares = jnp.exp(shifted - top)
        total = jnp.sum(shares, axis=0, keepdims=True)
        inverse = 1.0 / total
        yield
        mixed = dot(shares.astype(bf16), v_all, 0, 0)
        yield
        attended = [t.astype(bf16) for t in merge(mixed / as_column(total))]
        for x in range(2):
            out_ref[band * 2 + x, 0, inner] = attended[x]
        tall = jnp.concatenate([t.astype(f32) for t in attended for _ in range(2)], 0)
        products = g_two.astype(f32) * tall
        delta = jnp.sum(jnp.transpose(products), axis=0, keepdims=True)
        stat_ref[0, pl.ds(r, 1)] = top + jnp.log(total)
        stat_ref[1, pl.ds(r, 1)] = delta
        yield
        probs = shares * inverse
        slopes = (probs * (grad_probs - delta)).astype(bf16)
        probs = probs.astype(bf16)
        yield
        dq = merge(dot(slopes, k_all, 0, 0) * HEAD**-0.5)
        for x in range(2):
            out_ref[band * 2 + x, 1, inner] = dq[x].astype(bf16)
        yield
        for kv, left, two in ((0, slopes, q_two), (1, probs, g_two)):
            inside = dot(left[: 6 * SLOT], two, 1, 0)
            for a in range(3):
                for x in range(2):
                    at = (2 * a + x) * SLOT
                    acc[kv, r + a, x] += inside[at : at + SLOT]

    interleaved(line, rows)


def rim_kernel(rows, band_rows, me_ref, bias_ref, ext, sum_ref, west_ref, east_ref,
               west_stat, east_stat, *refs):
    block_refs = refs[:CHUNKS]
    cap_ref, acc = refs[CHUNKS:]
    me = me_ref[0]
    masks = head_masks()
    pad = pad_rows()
    from_east = lax.broadcasted_iota(jnp.int32, (1, WIDTH), 1) < HALF
    acc[...] = sum_ref[...]

    def line(r):
        band, inner = r // band_rows, r % band_rows
        scale = jnp.asarray(HEAD**-0.5, bf16)
        q_split = stacked([ref[band, 0, inner] * scale for ref in (east_ref, west_ref)], masks)[1]
        g_split = stacked([ref[band, 1, inner] for ref in (east_ref, west_ref)], masks)[1]
        k_own, v_own = [
            jnp.concatenate(
                [jnp.concatenate([ext[kv, r + a, 2], ext[kv, r + a, 1]], 1) for a in range(3)], 0
            )
            for kv in range(2)
        ]
        lse, delta = [
            jnp.where(from_east, east_stat[s, pl.ds(r, 1)], west_stat[s, pl.ds(r, 1)])
            for s in range(2)
        ]
        yield
        scores = dot(k_own, q_split, 1, 1)
        grad_probs = dot(v_own, g_split, 1, 1)
        yield
        shifted = biased(scores, [bias_ref[r, j : j + 1] for j in range(6, NPAIR)], pad)
        probs = jnp.exp(shifted - lse)
        slopes = (probs * (grad_probs - delta)).astype(bf16)
        probs = probs.astype(bf16)
        yield
        for kv, left, split in ((0, slopes, q_split), (1, probs, g_split)):
            part = dot(left, split, 1, 0)
            for a in range(3):
                acc[kv, r + a, 1] += part[a * SLOT : (a + 1) * SLOT, :LANES]
                acc[kv, r + a, 0] += part[a * SLOT : (a + 1) * SLOT, LANES:]

    interleaved(line, rows)
    for o, ref in enumerate(block_refs):
        target = me ^ o
        for kv in range(2):
            for i in range(band_rows):
                row = (target >> 1) * band_rows + i + 1
                ref[kv, i] = acc[kv, row, target & 1].astype(bf16)
    for end in range(2):
        for kv in range(2):
            cap_ref[end, kv] = acc[kv, end * (rows + 1)].astype(bf16)


def shift(value, axis, by, wrap):
    size = lax.axis_size(axis)
    pairs = [(i, (i + by) % size) for i in range(size) if wrap or 0 <= i + by < size]
    return lax.ppermute(value, axis, pairs)


def crossed(value, by):
    count, inner = lax.axis_size("lon_out"), lax.axis_size("lon_in")
    pairs = []
    for z in range(count):
        for x in range(inner):
            there = (z + (by if x == 0 else -by)) % count
            pairs.append((z * inner + x, there * inner + x))
    return lax.ppermute(value, ("lon_out", "lon_in"), pairs)


def swapped(blocks):
    out = [None] * CHUNKS
    out[0] = blocks[0]
    for o in ROUTES:
        out[o] = lax.ppermute(blocks[o], GROUP, [(i, i ^ o) for i in range(CHUNKS)])
    return out


def packed(first, second):
    both = jnp.stack([first, second])
    both = jnp.pad(both, ((0, 0), (0, 0), (0, SLOT - TILE), (0, 0)))
    split = both.reshape(both.shape[:3] + (both.shape[3] // LANES, LANES))
    return split.transpose(3, 0, 1, 2, 4)


def unpacked(block):
    moved = block.transpose(1, 2, 3, 0, 4)
    joined = moved.reshape(moved.shape[:3] + (moved.shape[3] * LANES,))
    return joined[:, :, :TILE]


def bias_table(pair_list, quad_index, quad_table, first_row, rows):
    lat_count = pair_list.shape[0]
    own_row = first_row + jnp.arange(rows, dtype=jnp.int32)
    code = jnp.arange(NPAIR, dtype=jnp.int32)
    if lat_count > rows:
        pairs = lax.dynamic_slice_in_dim(pair_list, first_row, rows, 0)
    else:
        pairs = pair_list
    listed = jnp.any(pairs[:, :, None] == code, axis=1)
    source = own_row[:, None] + code // 3 - 1
    pick = source[..., None] == jnp.arange(lat_count, dtype=jnp.int32)
    entry = jnp.sum(jnp.where(pick, quad_index, 0), axis=2)
    pick = entry[..., None] == jnp.arange(quad_table.shape[0], dtype=jnp.int32)
    weight = jnp.sum(jnp.where(pick, quad_table, 0.0), axis=2)
    bias = jnp.where(listed, jnp.log(weight), FAR).reshape(rows, 3, 3)
    first = jnp.concatenate([bias[:, :, 1:].reshape(rows, 6), bias[:, :, 0]], 1)
    second = jnp.concatenate([bias[:, :, :2].reshape(rows, 6), bias[:, :, 2]], 1)
    lane = jnp.arange(WIDTH, dtype=jnp.int32)
    return jnp.where(lane < HALF, first[:, :, None], second[:, :, None])


def on_device(queries, keys, values, cotangent, pair_list, quad_index, quad_table):
    band_rows = queries.shape[0]
    bands = lax.axis_size("lat_in")
    rows = band_rows * bands
    lat_groups = lax.axis_size("lat_out")
    me = lax.axis_index(GROUP).astype(jnp.int32)
    me_list = me.reshape(1)
    smem = pl.BlockSpec(memory_space=pltpu.SMEM)
    vmem = pl.BlockSpec(memory_space=pltpu.VMEM)
    params = pltpu.CompilerParams(vmem_limit_bytes=32 * 2**20)
    block = jax.ShapeDtypeStruct((2, band_rows, SLOT, LANES), bf16)
    natural = jnp.arange(CHUNKS, dtype=jnp.int32) ^ me

    def exchange(value):
        return lax.all_to_all(value, GROUP, 0, 0, tiled=True)

    def halves(value):
        return value.reshape((bands, 2) + value.shape[1:])

    blocks = pl.pallas_call(
        pack_kernel,
        out_shape=(block,) * CHUNKS,
        in_specs=[smem, vmem, vmem],
        out_specs=(vmem,) * CHUNKS,
        compiler_params=params,
        name="pack_keys",
    )(me_list, keys, values)
    blocks = swapped(blocks)
    odd = crossed(jnp.stack(blocks[1::2]), 1)
    even = crossed(jnp.stack(blocks[0::2]), -1)
    qg = exchange(packed(queries, cotangent))
    west = shift(halves(qg)[:, 1], "lon_out", 1, True)
    east = shift(halves(qg)[:, 0], "lon_out", -1, True)
    if lat_groups > 1:
        whole = halves(jnp.stack(blocks)[natural])
        spot = natural[::2] // 2
        odd_n, even_n = odd[spot], even[spot]
        left = jnp.where(me % 2 == 0, odd_n, even_n)
        right = jnp.where(me % 2 == 0, even_n, odd_n)

        def edge(band, inner):
            tiles = [left[band, :, inner], whole[band, 0, :, inner],
                     whole[band, 1, :, inner], right[band, :, inner]]
            return jnp.stack(tiles, 1)

        north = shift(edge(bands - 1, band_rows - 1), "lat_out", 1, False)
        south = shift(edge(0, 0), "lat_out", -1, False)
        caps = jnp.stack([north, south])
        first_row = (lax.axis_index("lat_out") * rows).astype(jnp.int32)
    else:
        caps = jnp.zeros((2, 2, 4, SLOT, LANES), bf16)
        first_row = 0
    bias = bias_table(pair_list, quad_index, quad_table, first_row, rows)
    out, acc, ext, stats = pl.pallas_call(
        functools.partial(main_kernel, rows, band_rows),
        out_shape=(
            jax.ShapeDtypeStruct(qg.shape, bf16),
            jax.ShapeDtypeStruct((2, rows + 2, 2, SLOT, LANES), f32),
            jax.ShapeDtypeStruct((2, rows + 2, 4, SLOT, LANES), bf16),
            jax.ShapeDtypeStruct((2, rows, WIDTH), f32),
        ),
        in_specs=[smem] + [vmem] * (5 + CHUNKS),
        out_specs=(vmem,) * 4,
        compiler_params=params,
        name="main_rows",
    )(me_list, bias, qg, odd, even, caps, *blocks)
    west_stat = shift(stats, "lon_out", 1, True)
    east_stat = shift(stats, "lon_out", -1, True)
    out = exchange(out)
    grads = pl.pallas_call(
        functools.partial(rim_kernel, rows, band_rows),
        out_shape=(block,) * CHUNKS
        + (jax.ShapeDtypeStruct((2, 2, 2, SLOT, LANES), bf16),),
        in_specs=[smem] + [vmem] * 7,
        out_specs=(vmem,) * (CHUNKS + 1),
        scratch_shapes=[pltpu.VMEM(acc.shape, f32)],
        compiler_params=params,
        name="rim_rows",
    )(me_list, bias, ext, acc, west, east, west_stat, east_stat)
    blocks, cap = grads[:CHUNKS], grads[CHUNKS]
    if lat_groups > 1:
        north = shift(cap[1], "lat_out", 1, False).astype(f32)
        south = shift(cap[0], "lat_out", -1, False).astype(f32)
        whole = halves(jnp.stack(blocks)[natural]).astype(f32)
        for band, inner, add in ((0, 0, north), (bands - 1, band_rows - 1, south)):
            whole = whole.at[band, :, :, inner].add(add.swapaxes(0, 1))
        whole = whole.astype(bf16).reshape((CHUNKS,) + block.shape)[natural]
        blocks = [whole[o] for o in range(CHUNKS)]
    blocks = swapped(blocks)
    tile = jax.ShapeDtypeStruct(queries.shape, bf16)
    dk, dv = pl.pallas_call(
        unpack_kernel,
        out_shape=(tile, tile),
        in_specs=[smem] + [vmem] * CHUNKS,
        out_specs=(vmem, vmem),
        compiler_params=params,
        name="unpack_grads",
    )(me_list, *blocks)
    out = unpacked(out)
    return out[0], out[1], dk, dv


def solution(mesh):
    lat, lon = mesh.shape["lat"], mesh.shape["lon"]
    lon_in = LON_GROUP
    lat_in = CHUNKS // lon_in
    finer = Mesh(
        mesh.devices.reshape(lat // lat_in, lat_in, lon // lon_in, lon_in),
        ("lat_out", "lat_in", "lon_out", "lon_in"),
    )
    spec = P(("lat_out", "lat_in"), ("lon_out", "lon_in"), None)
    return jax.shard_map(
        on_device,
        mesh=finer,
        in_specs=(spec,) * 4 + (P(),) * 3,
        out_specs=(spec,) * 4,
        check_vma=False,
    )
```

```python
import functools
import jax
import jax.numpy as jnp
from jax import lax
from jax.experimental import pallas as pl
from jax.experimental.pallas import tpu as pltpu
from jax.sharding import Mesh, PartitionSpec as P

HEADS = 16
HEAD = 64
TILE = 45
NPAIR = 9
LANES = 128
SLOT = 48
HALF = 2 * SLOT
WIDTH = 2 * HALF
LON_GROUP = 2
CHUNKS = HEADS * HEAD // LANES
ROUTES = (5, 7, 4, 6, 1, 3, 2)
FAR = -1e30
GROUPED = 2
MAIN_BANDS = 4
RIM_BANDS = 4
GROUP = ("lat_in", "lon_in")


f32, bf16 = jnp.float32, jnp.bfloat16


def dot(a, b, da, db):
    return lax.dot_general(a, b, (((da,), (db,)), ((), ())), preferred_element_type=f32)


def pack_kernel(me_ref, held, *out_refs):
    me = me_ref[0]
    for o, out_ref in enumerate(out_refs):
        lanes = pl.ds(pl.multiple_of((me ^ o) * LANES, LANES), LANES)
        for kv in range(2):
            for i in range(held.shape[1]):
                out_ref[kv, i, 32:] = jnp.zeros((SLOT - 32, LANES), bf16)
                out_ref[kv, i, :TILE] = held[kv, i, :, lanes]


def unpack_kernel(me_ref, *refs):
    me = me_ref[0]
    held, sems = refs[CHUNKS + 2 :]
    copies = []
    for kv, out in enumerate(refs[CHUNKS : CHUNKS + 2]):
        for i in range(held.shape[1]):
            for o, block_ref in enumerate(refs[:CHUNKS]):
                lanes = pl.ds(pl.multiple_of((me ^ o) * LANES, LANES), LANES)
                held[kv, i, :, lanes] = block_ref[kv, i, :TILE]
            copies.append(pltpu.make_async_copy(held.at[kv, i], out.at[i], sems.at[kv, i]))
            copies[-1].start()
    for copy in copies:
        copy.wait()


def head_masks():
    low = lax.broadcasted_iota(jnp.int32, (SLOT, LANES), 1) < HEAD
    return low, low.astype(bf16), jnp.logical_not(low).astype(bf16)


def pad_rows():
    row = lax.broadcasted_iota(jnp.int32, (8, WIDTH), 0)
    return jnp.where(row < TILE - (SLOT - 8), 0.0, FAR)


def stacked(pair, masks):
    tall = [jnp.concatenate([t * masks[1], t * masks[2]], 0) for t in pair]
    blank = jnp.zeros((HALF, LANES), bf16)
    split = [
        jnp.concatenate([tall[0], blank], 1),
        jnp.concatenate([blank, tall[1]], 1),
    ]
    return jnp.concatenate(tall, 0), jnp.concatenate(split, 0)


def biased(scores, rows, pad):
    parts = []
    for j, row in enumerate(rows):
        block = scores[j * SLOT : (j + 1) * SLOT]
        parts += [block[: SLOT - 8] + row, block[SLOT - 8 :] + (row + pad)]
    return jnp.concatenate(parts, 0)


def interleaved(line, rows, flight):
    def step(i, carry):
        waiting = [line(i * flight + k, k) for k in range(flight)]
        live = []
        while waiting or live:
            if waiting:
                live.append(waiting.pop(0))
            live = [one for one in live if next(one, FAR) != FAR]
        return carry

    lax.fori_loop(0, rows // flight, step, 0)


def main_kernel(rows, band_rows, me_ref, bias_ref, qg_ref, own_odd, own_even, odd_ref, even_ref,
                cap_ref, out_hbm, acc, stat_ref, ext, out_ref, sems):
    me = me_ref[0]
    side = me & 1

    def place(ref, j, o, tile):
        for i in range(band_rows):
            row = ((me ^ o) >> 1) * band_rows + i + 1
            for kv in range(2):
                ext[kv, row, tile] = ref[j, kv, i]

    for j in range(CHUNKS // 2):
        odd, even = 2 * j + 1, 2 * j
        place(own_odd, j, odd, 2 - side)
        place(own_even, j, even, 1 + side)
        place(odd_ref, j, odd, 3 * side)
        place(even_ref, j, even, 3 - 3 * side)
    for end in range(2):
        for kv in range(2):
            ext[kv, end * (rows + 1)] = cap_ref[end, kv]
    acc[...] = jnp.zeros_like(acc)
    masks = head_masks()
    pad = pad_rows()

    def merge(full):
        tiles = []
        for x in range(2):
            part = full[x * HALF : (x + 1) * HALF, x * LANES : (x + 1) * LANES]
            tiles.append(jnp.where(masks[0], part[:SLOT], part[SLOT:]))
        return tiles

    def as_column(row):
        return jnp.transpose(jnp.broadcast_to(row, (8, WIDTH)))[:, :1]

    def gathered(kv, r):
        inside = jnp.concatenate([ext[kv, r + a, x] for a in range(3) for x in (1, 2)], 0)
        rim = jnp.concatenate(
            [jnp.concatenate([ext[kv, r + a, 0], ext[kv, r + a, 3]], 1) for a in range(3)], 0
        )
        return jnp.concatenate([jnp.concatenate([inside, inside], 1), rim], 0)

    def line(r, k):
        band, inner = r // band_rows, r % band_rows
        scale = jnp.asarray(HEAD**-0.5, bf16)
        q_two, q_split = stacked([qg_ref[band * 2 + x, 0, inner] * scale for x in range(2)], masks)
        g_two, g_split = stacked([qg_ref[band * 2 + x, 1, inner] for x in range(2)], masks)
        k_all, v_all = gathered(0, r), gathered(1, r)
        yield
        scores = dot(k_all, q_split, 1, 1)
        grad_probs = dot(v_all, g_split, 1, 1)
        yield
        shifted = biased(scores, [bias_ref[r, j : j + 1] for j in range(NPAIR)], pad)
        top = jnp.max(shifted, axis=0, keepdims=True)
        yield
        shares = jnp.exp(shifted - top)
        total = jnp.sum(shares, axis=0, keepdims=True)
        inverse = 1.0 / total
        yield
        mixed = dot(shares.astype(bf16), v_all, 0, 0)
        yield
        attended = [t.astype(bf16) for t in merge(mixed / as_column(total))]
        for x in range(2):
            out_ref[band * 2 + x, 0, inner] = attended[x]
        tall = jnp.concatenate([t.astype(f32) for t in attended for _ in range(2)], 0)
        products = g_two.astype(f32) * tall
        delta = jnp.sum(jnp.transpose(products), axis=0, keepdims=True)
        stat_ref[0, pl.ds(r, 1)] = top + jnp.log(total)
        stat_ref[1, pl.ds(r, 1)] = delta
        yield
        probs = shares * inverse
        slopes = (probs * (grad_probs - delta)).astype(bf16)
        probs = probs.astype(bf16)
        yield
        dq = merge(dot(slopes, k_all, 0, 0) * HEAD**-0.5)
        for x in range(2):
            out_ref[band * 2 + x, 1, inner] = dq[x].astype(bf16)
        for kv, left, two in ((0, slopes, q_two), (1, probs, g_two)):
            inside = dot(left[: 6 * SLOT], two, 1, 0)
            for a in range(3):
                for x in range(2):
                    at = (2 * a + x) * SLOT
                    acc[kv, r + a, x] += inside[at : at + SLOT]
        if k % band_rows == band_rows - 1:
            send(band).start()

    def send(group):
        part = pl.ds(group * GROUPED, GROUPED)
        return pltpu.make_async_copy(
            out_ref.at[part], out_hbm.at[part], sems.at[group]
        )

    flight = MAIN_BANDS * band_rows if rows % (MAIN_BANDS * band_rows) == 0 else band_rows

    interleaved(line, rows, flight)
    for band in range(rows // band_rows):
        send(band).wait()


def rim_kernel(rows, band_rows, capped, me_ref, bias_ref, own_even, own_odd, edge_ref, sum_ref,
               east_hbm, west_hbm, stat_ref, *refs):
    block_refs = refs[:CHUNKS]
    acc, ext, guest_ref, sems = refs[-4:]
    me = me_ref[0]
    bands = rows // band_rows

    def guest(e, band):
        ref = (east_hbm, west_hbm)[e]
        at = sems.at[e * bands + band]
        return pltpu.make_async_copy(ref.at[band], guest_ref.at[e, band], at)

    for band in range(min(2, bands)):
        for e in range(2):
            guest(e, band).start()
    for o in range(CHUNKS):
        for i in range(band_rows):
            row = ((me ^ o) >> 1) * band_rows + i + 1
            for kv in range(2):
                ext[kv, row, (me ^ o) & 1] = (own_even, own_odd)[o & 1][o >> 1, kv, i]
    for kv in range(2):
        for end in range(2):
            for x in range(2):
                ext[kv, end * (rows + 1), x] = edge_ref[end, kv, x]
    masks = head_masks()
    pad = pad_rows()
    acc[...] = sum_ref[...]

    def line(r, k):
        band, inner = r // band_rows, r % band_rows
        if k % band_rows == 0:
            for e in range(2):
                guest(e, band).wait()

            @pl.when(band + 2 < bands)
            def _():
                for e in range(2):
                    guest(e, jnp.minimum(band + 2, bands - 1)).start()

        scale = jnp.asarray(HEAD**-0.5, bf16)
        q_split = stacked([guest_ref[e, band, 0, inner] * scale for e in range(2)], masks)[1]
        g_split = stacked([guest_ref[e, band, 1, inner] for e in range(2)], masks)[1]
        k_own, v_own = [
            jnp.concatenate(
                [jnp.concatenate([ext[kv, r + a, x] for x in (1, 0)], 1) for a in range(3)], 0
            )
            for kv in range(2)
        ]
        lse, delta = [stat_ref[s, pl.ds(r, 1)] for s in range(2)]
        yield
        scores = dot(k_own, q_split, 1, 1)
        grad_probs = dot(v_own, g_split, 1, 1)
        yield
        shifted = biased(scores, [bias_ref[r, j : j + 1] for j in range(6, NPAIR)], pad)
        probs = jnp.exp(shifted - lse)
        slopes = (probs * (grad_probs - delta)).astype(bf16)
        probs = probs.astype(bf16)
        yield
        for kv, left, split in ((0, slopes, q_split), (1, probs, g_split)):
            part = dot(left, split, 1, 0)
            for a in range(3):
                acc[kv, r + a, 1] += part[a * SLOT : (a + 1) * SLOT, :LANES]
                acc[kv, r + a, 0] += part[a * SLOT : (a + 1) * SLOT, LANES:]

    flight = RIM_BANDS * band_rows if rows % (RIM_BANDS * band_rows) == 0 else band_rows

    interleaved(line, rows, flight)
    for o, ref in enumerate(block_refs):
        target = me ^ o
        for kv in range(2):
            for i in range(band_rows):
                row = (target >> 1) * band_rows + i + 1
                ref[kv, i] = acc[kv, row, target & 1].astype(bf16)
    if capped:
        for end in range(2):
            for kv in range(2):
                refs[CHUNKS][end, kv] = acc[kv, end * (rows + 1)].astype(bf16)


def shift(value, axis, by, wrap):
    size = lax.axis_size(axis)
    pairs = [(i, (i + by) % size) for i in range(size) if wrap or 0 <= i + by < size]
    return lax.ppermute(value, axis, pairs)


def crossed(value, by):
    count, inner = lax.axis_size("lon_out"), lax.axis_size("lon_in")
    pairs = []
    for z in range(count):
        for x in range(inner):
            there = (z + (by if x == 0 else -by)) % count
            pairs.append((z * inner + x, there * inner + x))
    return lax.ppermute(value, ("lon_out", "lon_in"), pairs)


def swapped(blocks):
    out = [None] * CHUNKS
    out[0] = blocks[0]
    for o in ROUTES:
        out[o] = lax.ppermute(blocks[o], GROUP, [(i, i ^ o) for i in range(CHUNKS)])
    return out


def packed(first, second):
    both = jnp.stack([first, second])
    both = jnp.pad(both, ((0, 0), (0, 0), (0, SLOT - TILE), (0, 0)))
    split = both.reshape(both.shape[:3] + (both.shape[3] // LANES, LANES))
    return split.transpose(3, 0, 1, 2, 4)


def unpacked(block):
    moved = block.transpose(1, 2, 3, 0, 4)
    joined = moved.reshape(moved.shape[:3] + (moved.shape[3] * LANES,))
    return joined[:, :, :TILE]


def bias_table(pair_list, quad_index, quad_table, first_row, rows):
    lat_count = pair_list.shape[0]
    own_row = first_row + jnp.arange(rows, dtype=jnp.int32)
    code = jnp.arange(NPAIR, dtype=jnp.int32)
    if lat_count > rows:
        pairs = lax.dynamic_slice_in_dim(pair_list, first_row, rows, 0)
    else:
        pairs = pair_list
    listed = jnp.any(pairs[:, :, None] == code, axis=1)
    source = own_row[:, None] + code // 3 - 1
    pick = source[..., None] == jnp.arange(lat_count, dtype=jnp.int32)
    entry = jnp.sum(jnp.where(pick, quad_index, 0), axis=2)
    pick = entry[..., None] == jnp.arange(quad_table.shape[0], dtype=jnp.int32)
    weight = jnp.sum(jnp.where(pick, quad_table, 0.0), axis=2)
    bias = jnp.where(listed, jnp.log(weight), FAR).reshape(rows, 3, 3)
    first = jnp.concatenate([bias[:, :, 1:].reshape(rows, 6), bias[:, :, 0]], 1)
    second = jnp.concatenate([bias[:, :, :2].reshape(rows, 6), bias[:, :, 2]], 1)
    lane = jnp.arange(WIDTH, dtype=jnp.int32)
    return jnp.where(lane < HALF, first[:, :, None], second[:, :, None])


def on_device(queries, keys, values, cotangent, pair_list, quad_index, quad_table):
    band_rows = queries.shape[0]
    bands = lax.axis_size("lat_in")
    rows = band_rows * bands
    lat_groups = lax.axis_size("lat_out")
    me = lax.axis_index(GROUP).astype(jnp.int32)
    me_list = me.reshape(1)
    smem = pl.BlockSpec(memory_space=pltpu.SMEM)
    vmem = pl.BlockSpec(memory_space=pltpu.VMEM)
    anywhere = pl.BlockSpec(memory_space=pl.ANY)
    params = pltpu.CompilerParams(vmem_limit_bytes=16 * 2**20)
    block = jax.ShapeDtypeStruct((2, band_rows, SLOT, LANES), bf16)
    natural = jnp.arange(CHUNKS, dtype=jnp.int32) ^ me

    def exchange(value):
        return lax.all_to_all(value, GROUP, 0, 0, tiled=True)

    def halves(value):
        return value.reshape((bands, 2) + value.shape[1:])

    blocks = pl.pallas_call(
        pack_kernel,
        out_shape=(block,) * CHUNKS,
        in_specs=[smem, vmem],
        out_specs=(vmem,) * CHUNKS,
        compiler_params=params,
        name="pack_keys",
    )(me_list, jnp.stack([keys, values]))
    blocks = swapped(blocks)
    own_odd, own_even = jnp.stack(blocks[1::2]), jnp.stack(blocks[0::2])
    odd, even = crossed(own_odd, 1), crossed(own_even, -1)
    qg = exchange(packed(queries, cotangent))
    west = shift(halves(qg)[:, 1], "lon_out", 1, True)
    east = shift(halves(qg)[:, 0], "lon_out", -1, True)
    if lat_groups > 1:
        whole = halves(jnp.stack(blocks)[natural])
        spot = natural[::2] // 2
        odd_n, even_n = odd[spot], even[spot]
        left = jnp.where(me % 2 == 0, odd_n, even_n)
        right = jnp.where(me % 2 == 0, even_n, odd_n)

        def edge(band, inner):
            tiles = [left[band, :, inner], whole[band, 0, :, inner],
                     whole[band, 1, :, inner], right[band, :, inner]]
            return jnp.stack(tiles, 1)

        north = shift(edge(bands - 1, band_rows - 1), "lat_out", 1, False)
        south = shift(edge(0, 0), "lat_out", -1, False)
        caps = jnp.stack([north, south])
        first_row = (lax.axis_index("lat_out") * rows).astype(jnp.int32)
    else:
        caps = jnp.zeros((2, 2, 4, SLOT, LANES), bf16)
        first_row = 0
    bias = bias_table(pair_list, quad_index, quad_table, first_row, rows)
    out, acc, stats = pl.pallas_call(
        functools.partial(main_kernel, rows, band_rows),
        out_shape=(
            jax.ShapeDtypeStruct(qg.shape, bf16),
            jax.ShapeDtypeStruct((2, rows + 3, 2, SLOT, LANES), f32),
            jax.ShapeDtypeStruct((2, rows, WIDTH), f32),
        ),
        in_specs=[smem] + [vmem] * 7,
        out_specs=(anywhere, vmem, vmem),
        scratch_shapes=[
            pltpu.VMEM((2, rows + 2, 4, SLOT, LANES), bf16),
            pltpu.VMEM(qg.shape, bf16),
            pltpu.SemaphoreType.DMA((bands,)),
        ],
        compiler_params=params,
        name="main_rows",
    )(me_list, bias, qg, own_odd, own_even, odd, even, caps)
    from_west = shift(stats, "lon_out", 1, True)
    from_east = shift(stats, "lon_out", -1, True)
    lane = jnp.arange(WIDTH, dtype=jnp.int32)
    stats = jnp.where(lane < HALF, from_east, from_west)
    out = exchange(out)
    cap_shape = (jax.ShapeDtypeStruct((2, 2, 2, SLOT, LANES), bf16),)
    cap_shape = cap_shape if lat_groups > 1 else ()
    grads = pl.pallas_call(
        functools.partial(rim_kernel, rows, band_rows, lat_groups > 1),
        out_shape=(block,) * CHUNKS + cap_shape,
        in_specs=[smem] + [vmem] * 5 + [anywhere] * 2 + [vmem],
        out_specs=(vmem,) * (CHUNKS + len(cap_shape)),
        scratch_shapes=[
            pltpu.VMEM((2, rows + 2, 2, SLOT, LANES), t) for t in (f32, bf16)
        ]
        + [pltpu.VMEM((2,) + west.shape, bf16), pltpu.SemaphoreType.DMA((2 * bands,))],
        compiler_params=params,
        name="rim_rows",
    )(me_list, bias, own_even, own_odd, caps[:, :, 1:3], acc[:, : rows + 2], east, west, stats)
    blocks = grads[:CHUNKS]
    if lat_groups > 1:
        cap = grads[CHUNKS]
        north = shift(cap[1], "lat_out", 1, False).astype(f32)
        south = shift(cap[0], "lat_out", -1, False).astype(f32)
        whole = halves(jnp.stack(blocks)[natural]).astype(f32)
        for band, inner, add in ((0, 0, north), (bands - 1, band_rows - 1, south)):
            whole = whole.at[band, :, :, inner].add(add.swapaxes(0, 1))
        whole = whole.astype(bf16).reshape((CHUNKS,) + block.shape)[natural]
        blocks = [whole[o] for o in range(CHUNKS)]
    blocks = swapped(blocks)
    tile = jax.ShapeDtypeStruct(queries.shape, bf16)
    dk, dv = pl.pallas_call(
        unpack_kernel,
        out_shape=(tile, tile),
        in_specs=[smem] + [vmem] * CHUNKS,
        out_specs=(anywhere, anywhere),
        scratch_shapes=[
            pltpu.VMEM((2,) + queries.shape, bf16),
            pltpu.SemaphoreType.DMA((2, band_rows)),
        ],
        compiler_params=params,
        name="unpack_grads",
    )(me_list, *blocks)
    out = unpacked(out)
    return out[0], out[1], dk, dv


def solution(mesh):
    lat, lon = mesh.shape["lat"], mesh.shape["lon"]
    lon_in = LON_GROUP
    lat_in = CHUNKS // lon_in
    finer = Mesh(
        mesh.devices.reshape(lat // lat_in, lat_in, lon // lon_in, lon_in),
        ("lat_out", "lat_in", "lon_out", "lon_in"),
    )
    spec = P(("lat_out", "lat_in"), ("lon_out", "lon_in"), None)
    return jax.shard_map(
        on_device,
        mesh=finer,
        in_specs=(spec,) * 4 + (P(),) * 3,
        out_specs=(spec,) * 4,
        check_vma=False,
    )
```
